128 devices in a mesh: region: 64 (over z, y, x_hi, core), sub: 2 (over x_lo).
Axes of the slice: x: 4 (x_hi: 2, x_lo: 2; x = x_hi * 2 + x_lo), y: 4, z: 4, core: 2. Of those that a mesh axis runs over, the one named last changes fastest.
Arguments:
- sources: bfloat16 [128, 2048, 1280], P(('region', 'sub')), may hold values from -6 to 6
- coupling: bfloat16 [128, 2048, 2048], P(('region', 'sub')), may hold values from -0.0625 to 0.0625
- self_term: float32 [128, 2048], P(('region', 'sub')), may hold values from 0.25 to 1
- history: float32 [128, 4, 8, 640], P(('region', 'sub')), may hold values from -6 to 6
- line_nodes: int32 [128, 4, 8], P(('region', 'sub')), may hold values from -1 to 2047, as said below
- line_admit: float32 [128, 4, 8], P(('region', 'sub')), may hold values from 0 to 1, as said below
- term_region: int32 [32768, 1], P(('region', 'sub')), may hold values from 0 to 63; in each aligned block of 256 rows (0 to 255, 256 to 511, ...) at most 8 rows name the same one
- old_samples: bfloat16 [32768, 1280], P(('region', 'sub')), may hold values from -6 to 6
- prior_phasor: float32 [32768, 2, 128], P(('region', 'sub')), may hold values from -6 to 6
Outputs:
- next_history: float32 [128, 4, 8, 640], P(('region', 'sub'))
- node_voltages: bfloat16 [128, 2048, 1280], P(('region', 'sub'))
- phasors: float32 [65536, 2, 2, 128], P(('region', 'sub'))
The draws below stay inside these ranges and needn't reach their ends.
Inputs may be any that keep to these rules, and one draw needn't show every extreme that they name: line_nodes[a, d, k] is -1 for an empty slot and for every slot of a direction with no subsystem; each subsystem has lines to each of its up to 4 neighbours in the directions of the steps, 1 to 8 lines a pair, in the first slots; [a, d, k] and the slot k of the opposite direction at the neighbour are both -1 or are the two ends of one line; some pair uses all 8 slots. line_admit is equal at the two ends of a line; it is 0 exactly where line_nodes is -1, else 0.25 or more. `term_region`: among the 256 terminals of one subsystem at most 8 name the same region, and in every draw some region is named by exactly 8 of one subsystem's terminals.
All inputs are finite; a program needn't handle non-finite values.
Results may differ from the reference program's by a relative error of at most 0.003.
Values sent between devices are 32-bit elements; how exact they have to be, the bound alone decides.
A program may use at most 128 MiB of HBM per device.

```python
import math
import jax
import jax.numpy as jnp
import numpy as np
from jax import lax

NODES = 2048
NEIGH = 4
LPP = 8
DELAY = 40
SPANS = 2
SCEN = 16
TERM_DEV = 256
BINS = 8
DFT_LEN = 2048
SUBSYSTEMS = 128
STEPS = 80
CAP = 8
TERMINALS = 32768
N_REGION = 64
N_SUB = 2


def spread_edges(sub_edges, region_edges):
    sub_pad = jnp.pad(sub_edges, ((0, 0), (1, 1)) + ((0, 0),) * (sub_edges.ndim - 2))
    region_pad = jnp.pad(region_edges, ((1, 1), (0, 0)) + ((0, 0),) * (region_edges.ndim - 2))
    toward_lower_sub = sub_pad[:, :N_SUB]
    toward_upper_sub = sub_pad[:, 1:N_SUB + 1]
    toward_lower_region = region_pad[:N_REGION]
    toward_upper_region = region_pad[1:N_REGION + 1]
    stacked = jnp.stack([toward_lower_sub, toward_upper_sub, toward_lower_region, toward_upper_region], axis=2)
    return stacked.reshape((N_REGION * N_SUB, NEIGH) + stacked.shape[3:])


def line_tables(key):
    key_subc = jax.random.fold_in(key, 21)
    key_regc = jax.random.fold_in(key, 22)
    key_pick = jax.random.fold_in(key, 23)
    key_nodes = jax.random.fold_in(key, 24)
    key_suba = jax.random.fold_in(key, 25)
    key_rega = jax.random.fold_in(key, 26)
    sub_counts = jax.random.randint(key_subc, (N_REGION, N_SUB - 1), 1, LPP + 1)
    region_counts = jax.random.randint(key_regc, (N_REGION - 1, N_SUB), 1, LPP + 1)
    chosen = jax.random.randint(key_pick, (), 0, N_REGION * (N_SUB - 1))
    flat_index = jnp.arange(N_REGION * (N_SUB - 1)).reshape(N_REGION, N_SUB - 1)
    sub_counts = jnp.where(flat_index == chosen, LPP, sub_counts)
    counts = spread_edges(sub_counts, region_counts)
    slots = jnp.arange(LPP)
    live_slot = slots[None, None, :] < counts[:, :, None]
    end_nodes = jax.random.randint(key_nodes, (N_REGION * N_SUB, NEIGH, LPP), 0, NODES)
    end_nodes = jnp.where(live_slot, end_nodes, -1).astype(jnp.int32)
    sub_admit = jax.random.uniform(key_suba, (N_REGION, N_SUB - 1, LPP), jnp.float32)
    region_admit = jax.random.uniform(key_rega, (N_REGION - 1, N_SUB, LPP), jnp.float32)
    mirrored = spread_edges(sub_admit, region_admit)
    admit = jnp.where(live_slot, 0.25 * jnp.exp(jnp.log(4.0) * mirrored), 0.0).astype(jnp.float32)
    return (end_nodes, admit)


def draw_line_nodes(key, part):
    return line_tables(key)[0]


def draw_line_admit(key, part):
    return line_tables(key)[1]


def block_levels(key, shape, cuts, least, top_value):
    def one(axis_at, blocks):
        draws = jax.random.uniform(jax.random.fold_in(jax.random.fold_in(key, 6), axis_at), (blocks,), jnp.float32, least / len(cuts), top_value / len(cuts))
        return jnp.repeat(jnp.exp(draws), shape[axis_at] // blocks).reshape((-1,) + (1,) * (len(shape) - axis_at - 1))

    factor_of = one(*cuts[0])
    for cut in cuts[1:]:
        factor_of = factor_of * one(*cut)
    return factor_of


def routed_block(own_key, own, number, rows, number_of, top, reach, lean):
    order = jax.random.permutation(own_key, number_of)
    heavy_load, ordinary = shares(number_of, rows * top, reach, lean, True), shares(number_of, rows * top, reach, lean, False)
    places = jnp.arange(number_of)

    def named(lengths, offset_by):
        used = int((lengths > 0).sum())
        fixed = max(1, used // 4)
        moved = fixed + (places - fixed + offset_by * (used - fixed)) % max(1, number_of - fixed)
        return jnp.zeros((number_of,), jnp.int32).at[order[jnp.where(places < fixed, places, moved)]].set(jnp.asarray(lengths, jnp.int32))

    lengths = jnp.where(number % 4 == 0, named(heavy_load, number // 4), named(ordinary, number - number // 4 - 1))
    mixed = jax.random.permutation(jax.random.fold_in(own, 3), number_of)
    donor, receiver = mixed[0:number_of // 2 * 2:2], mixed[1:number_of // 2 * 2:2]
    slack = jnp.minimum(lengths[donor] - 1, reach - lengths[receiver]) // 2
    slack = jnp.where((donor == order[0]) | (receiver == order[0]) | (lengths[receiver] == 0), 0, jnp.maximum(slack, 0))
    moved = jax.random.randint(jax.random.fold_in(own, 4), (number_of // 2,), 0, 1 << 20) % (slack + 1)
    lengths = lengths.at[donor].add(-moved).at[receiver].add(moved)
    items = jnp.searchsorted(jnp.cumsum(lengths), jnp.arange(rows * top), side="right").astype(jnp.int32)
    listing = items.reshape(top, rows).T
    listing = listing[jax.random.permutation(jax.random.fold_in(own, 1), rows)]
    offset_by = jax.random.randint(jax.random.fold_in(own, 2), (rows, 1), 0, top)
    return jnp.take_along_axis(listing, (jnp.arange(top)[None, :] + offset_by) % top, axis=1)


def shares(amount, total, bound, lean, full):
    weights = [(1 << 20) // math.isqrt(standing ** lean) + 1 for standing in range(1, amount + 1)]
    largest = bound if full else min(bound, max(-(-total // amount), total * weights[0] // sum(weights)))
    least = 1 if total - largest >= amount - 1 else 0
    given, spare = [largest] + [least] * (amount - 1), total - largest - least * (amount - 1)
    while spare > 0:
        free = [i for i in range(1, amount) if given[i] < largest] or [i for i in range(1, amount) if given[i] < bound]
        whole, left = sum([weights[i] for i in free]), spare
        for i in free:
            more = min(bound - given[i], max(1, left * weights[i] // whole), spare)
            given[i] = given[i] + more
            spare = spare - more
    return np.array(given)


def centred(rng, dims, spread, reach, cuts=(), held_as=jnp.bfloat16):
    array = spread * jax.random.normal(rng, dims, jnp.float32)
    if cuts:
        array = array * block_levels(rng, dims, cuts, -0.22, 0.18)
    return jnp.clip(array, -reach, reach).astype(held_as)


def setup_inputs(seed: int = 0) -> dict:
    arg_keys = jax.random.split(jax.random.key(seed), 10)
    sources = centred(arg_keys[0], (SUBSYSTEMS, NODES, STEPS * SCEN), 1.0, 6.0, ((0, 128),))
    coupling = centred(arg_keys[1], (SUBSYSTEMS, NODES, NODES), (4 * NODES) ** -0.5, 0.0625, ((0, 128),))
    self_term = jnp.clip(jnp.exp(math.log(1.0) - 1.3862944 * jax.random.uniform(arg_keys[2], (SUBSYSTEMS, NODES), jnp.float32) ** block_levels(arg_keys[2], (SUBSYSTEMS, NODES), ((0, 128),), -0.2, 0.2)), 0.25, 1.0)
    history = centred(arg_keys[3], (SUBSYSTEMS, NEIGH, LPP, DELAY * SCEN), 1.0, 6.0, ((0, 128),), jnp.float32)
    line_nodes = draw_line_nodes(jax.random.fold_in(arg_keys[9], 71), 0)
    line_admit = draw_line_admit(jax.random.fold_in(arg_keys[9], 71), 0)
    term_region_keys = jax.random.split(jax.random.fold_in(arg_keys[6], 1), TERMINALS // TERM_DEV)
    term_region_turns = jax.random.permutation(jax.random.fold_in(arg_keys[6], 3), TERMINALS // TERM_DEV)
    term_region = jax.vmap(lambda own, number: routed_block(jax.random.fold_in(arg_keys[6], 2), own, number, TERM_DEV, N_REGION, 1, CAP, 2))(term_region_keys, term_region_turns).reshape((TERMINALS, 1))
    old_samples = centred(arg_keys[7], (TERMINALS, STEPS * SCEN), 1.0, 6.0, ((0, 128),))
    prior_phasor = centred(arg_keys[8], (TERMINALS, 2, BINS * SCEN), 1.0, 6.0, ((0, 128),), jnp.float32)
    return dict(sources=sources, coupling=coupling, self_term=self_term, history=history, line_nodes=line_nodes, line_admit=line_admit, term_region=term_region, old_samples=old_samples, prior_phasor=prior_phasor)


def phasor_fit(differences, prior):
    row_count = differences.shape[0]
    blocks = differences.reshape(row_count, SPANS, DELAY, SCEN)
    step_index = jnp.arange(SPANS * DELAY, dtype=jnp.int32).reshape(SPANS, DELAY)
    harmonic = jnp.arange(1, BINS + 1, dtype=jnp.int32)
    product = step_index[:, :, None] * harmonic[None, None, :] % DFT_LEN
    angles = product.astype(differences.dtype) * (2.0 * math.pi / DFT_LEN)
    norm_scale = 1.0 / math.sqrt(DFT_LEN)
    twiddle = jnp.stack([jnp.cos(angles), -jnp.sin(angles)], axis=2) * norm_scale
    partial_value = jnp.einsum('ajts,jtch->ajchs', blocks, twiddle.astype(differences.dtype), precision=lax.Precision.HIGHEST)
    running = jnp.cumsum(partial_value, axis=1).reshape(row_count, SPANS, 2, BINS * SCEN)
    return running + prior[:, None]

def route_lines(outgoing):
    span_cols = outgoing.shape[-1]
    grid = outgoing.reshape(N_REGION, N_SUB, NEIGH, LPP, span_cols)
    no_pad = (0, 0)
    from_lower_sub = jnp.pad(grid[:, :-1, 1], (no_pad, (1, 0), no_pad, no_pad))
    from_upper_sub = jnp.pad(grid[:, 1:, 0], (no_pad, (0, 1), no_pad, no_pad))
    from_lower_region = jnp.pad(grid[:-1, :, 3], ((1, 0), no_pad, no_pad, no_pad))
    from_upper_region = jnp.pad(grid[1:, :, 2], ((0, 1), no_pad, no_pad, no_pad))
    arrived = jnp.stack([from_lower_sub, from_upper_sub, from_lower_region, from_upper_region], axis=2)
    return arrived.reshape(N_REGION * N_SUB, NEIGH, LPP, span_cols)

def reference(sources, coupling, self_term, history, line_nodes, line_admit, term_region, old_samples, prior_phasor):
    peers = N_REGION * N_SUB
    span_cols = DELAY * SCEN
    live_slot = line_nodes >= 0
    incoming = history
    pieces = []
    node_pieces = []
    for span_index in range(SPANS):
        span_src = sources[:, :, span_index * span_cols:(span_index + 1) * span_cols]

        def per_device(items):
            matrix, self_gain, block_src, arrived, end_nodes, live_row, admit_row = items
            end_flat = end_nodes.reshape(-1)
            live_flat = live_row.reshape(-1)
            line_rows = arrived.reshape(NEIGH * LPP, span_cols)
            target = jnp.where(live_flat, end_flat, NODES)
            injection = jnp.zeros((NODES, span_cols), jnp.float32).at[target].add(line_rows, mode='drop').astype(jnp.bfloat16)
            voltages = jnp.dot(matrix, block_src, preferred_element_type=jnp.float32)
            voltages = voltages + jnp.dot(matrix, injection, preferred_element_type=jnp.float32)
            voltages = voltages + self_gain[:, None] * (block_src.astype(jnp.float32) + injection.astype(jnp.float32))
            pick_rows = jnp.where(live_flat, end_flat, 0)
            line_volts = voltages[pick_rows]
            outgoing = jnp.where(live_flat[:, None], 2.0 * admit_row.reshape(-1, 1) * line_volts - line_rows, 0.0)
            return (outgoing.reshape(NEIGH, LPP, span_cols), voltages[:TERM_DEV], voltages.astype(jnp.bfloat16))
        outgoing, terminal_volts, all_volts = lax.map(per_device, (coupling, self_term, span_src, incoming, line_nodes, live_slot, line_admit))
        incoming = route_lines(outgoing)
        pieces.append(terminal_volts)
        node_pieces.append(all_volts)
    node_voltages = jnp.concatenate(node_pieces, axis=2)
    waveforms = jnp.concatenate(pieces, axis=2).reshape(peers * TERM_DEV, STEPS * SCEN)
    differences = waveforms - old_samples.astype(jnp.float32)
    fitted = phasor_fit(differences, prior_phasor)
    regions = term_region[:, 0].reshape(peers, TERM_DEV)
    onehot = (regions[:, :, None] == jnp.arange(N_REGION, dtype=jnp.int32)[None, None, :]).astype(jnp.int32)
    rank_in = jnp.cumsum(onehot, axis=1) - onehot
    slot_index = lax.optimization_barrier(jnp.sum(rank_in * onehot, axis=2))
    device_index = jnp.arange(peers, dtype=jnp.int32)[:, None]
    src_region = device_index // N_SUB
    src_sub = device_index % N_SUB
    dest_row = ((regions * N_SUB + src_sub) * N_REGION + src_region) * CAP + slot_index
    phasors = jnp.zeros((peers * N_REGION * CAP, SPANS, 2, BINS * SCEN), jnp.float32)
    phasors = phasors.at[dest_row.reshape(-1).astype(jnp.int32)].set(fitted)
    return (incoming, node_voltages, phasors)
```

```python
import math

import jax
import jax.numpy as jnp
import numpy as np
from jax import lax
from jax.experimental import pallas as pl
from jax.experimental.pallas import tpu as pltpu
from jax.sharding import PartitionSpec as P

NODES = 2048
NEIGH = 4
LPP = 8
SLOTS = NEIGH * LPP
DELAY = 40
SPANS = 2
SCEN = 16
TERM = 256
BINS = 8
DFT_LEN = 2048
COLS = DELAY * SCEN
WIDE = SPANS * COLS
REGIONS = 64
CAP = 8
BOX = REGIONS * CAP
LANES = 128
HARM = BINS * SCEN
PAD = 128
BLOCK = 256
SPLIT = 512
EARLY = 3
MESH = pl.DeviceIdType.MESH
F32 = jnp.float32
BF16 = jnp.bfloat16


def fit_tables():
    step = np.arange(SPANS * DELAY)
    bins = np.arange(1, BINS + 1)
    angle = (step[:, None] * bins[None, :] % DFT_LEN) * (2.0 * math.pi / DFT_LEN)
    wave = np.stack([np.cos(angle), -np.sin(angle)], axis=1) / math.sqrt(DFT_LEN)
    table = np.einsum("uch,st->uscht", wave, np.eye(SCEN))
    table = table.reshape(SPANS, COLS, 2 * HARM).astype(np.float32)
    high = table.astype(BF16)
    low = (table - high.astype(np.float32)).astype(BF16)
    return np.stack([high, low], axis=1)


def dot(a, b):
    return jnp.dot(a, b, preferred_element_type=F32)


def two(x):
    high = x.astype(BF16)
    return high, (x - high.astype(F32)).astype(BF16)


def stack4(*blocks):
    zero = jnp.zeros((SLOTS, blocks[0].shape[1]), BF16)
    blocks = blocks + (zero,) * (4 - len(blocks))
    return jnp.concatenate(blocks, axis=0)


def iota(shape, axis):
    return lax.broadcasted_iota(jnp.int32, shape, axis)


def kernel(
    nodes_ref,
    admit_ref,
    src_hbm,
    mat_hbm,
    old_hbm,
    prior_hbm,
    table_hbm,
    hist_ref,
    self_ref,
    region_ref,
    volt_ref,
    phasor_ref,
    next_ref,
    mat,
    rhs,
    old,
    prior,
    table,
    gain,
    picked,
    gathered,
    fresh,
    outgo,
    arrived,
    packed,
    landed,
    mat_sem,
    load_sem,
    line_send,
    line_recv,
    item_send,
    item_recv,
    own_sem,
):
    region = lax.axis_index("region")
    sub = lax.axis_index("sub")
    barrier = pltpu.get_barrier_semaphore()
    other_sub = {"region": region, "sub": 1 - sub}
    below = {"region": lax.rem(region + REGIONS - 1, REGIONS), "sub": sub}
    above = {"region": lax.rem(region + 1, REGIONS), "sub": sub}

    loads = [
        pltpu.make_async_copy(
            src_hbm.at[:, pl.ds(j * COLS, COLS)], rhs.at[:, pl.ds(PAD + j * COLS, COLS)], load_sem.at[j]
        )
        for j in range(SPANS)
    ]
    loads.append(pltpu.make_async_copy(old_hbm, old, load_sem.at[2]))
    loads.append(pltpu.make_async_copy(prior_hbm, prior, load_sem.at[3]))
    loads.append(pltpu.make_async_copy(table_hbm, table, load_sem.at[4]))
    mat_loads = [
        pltpu.make_async_copy(
            mat_hbm.at[pl.ds(i * BLOCK, BLOCK)], mat.at[pl.ds(i * BLOCK, BLOCK)], mat_sem.at[i]
        )
        for i in range(NODES // BLOCK)
    ]
    loads[0].start()
    mat_loads[0].start()
    loads[2].start()
    loads[3].start()
    loads[4].start()
    for load in mat_loads[1:]:
        load.start()
    loads[1].start()

    def greet(i, _):
        pl.semaphore_signal(
            barrier, inc=1, device_id={"region": lax.rem(region + i, REGIONS), "sub": sub}, device_id_type=MESH
        )
        return 0

    lax.fori_loop(1, REGIONS, greet, 0)
    pl.semaphore_signal(barrier, inc=1, device_id=other_sub, device_id_type=MESH)

    node_row = jnp.full((1, LANES), -1, jnp.int32)
    node_col = jnp.full((SLOTS, 1), -1, jnp.int32)
    admit_col = jnp.zeros((SLOTS, 1), F32)
    lane_slot = iota((1, LANES), 1) % SLOTS
    slot_id = iota((SLOTS, 1), 0)
    for k in range(SLOTS):
        node = nodes_ref[k // LPP, k % LPP]
        node_row = jnp.where(lane_slot == k, node, node_row)
        node_col = jnp.where(slot_id == k, node, node_col)
        admit_col = jnp.where(slot_id == k, admit_ref[k // LPP, k % LPP], admit_col)
    live = node_col >= 0
    same = (node_col == node_row) & live
    lane = iota((SLOTS, LANES), 1)
    earlier = jnp.where(same & (lane < slot_id), 1.0, 0.0)
    first = (jnp.sum(earlier, axis=1, keepdims=True) == 0.0) & live
    merge = jnp.where(same & (lane < 3 * SLOTS), 1.0, 0.0).astype(BF16)
    twice_admit = 2.0 * admit_col

    def line_injection(rows):
        high = rows.astype(BF16)
        rest = rows - high.astype(F32)
        mid = rest.astype(BF16)
        low = (rest - mid.astype(F32)).astype(BF16)
        total = dot(merge, stack4(high, mid, low))
        return jnp.where(first, total, 0.0).astype(BF16)

    def mark(i, _):
        rows = pl.ds(pl.multiple_of(i * BLOCK, BLOCK), BLOCK)
        number = iota((BLOCK, LANES), 0) + i * BLOCK
        rhs[rows, pl.ds(0, PAD)] = jnp.where(number == node_row, 1.0, 0.0).astype(BF16)
        diag = iota((BLOCK, BLOCK), 0) == iota((BLOCK, BLOCK), 1)
        gains = jnp.sum(jnp.where(diag, self_ref[:, rows], 0.0), axis=1, keepdims=True)
        gain[rows, :] = jnp.broadcast_to(gains, (BLOCK, LANES))
        return 0

    lax.fori_loop(0, NODES // BLOCK, mark, 0)
    chosen = jnp.where(node_col == iota((SLOTS, NODES), 1), 1.0, 0.0)
    line_gain = jnp.sum(chosen * self_ref[...], axis=1, keepdims=True)
    picked[SLOTS:, :] = chosen.astype(BF16)
    line_rows = hist_ref[...]
    injected = line_injection(line_rows)

    region_row = region_ref[...]
    square = (TERM, TERM)
    diag = iota(square, 0) == iota(square, 1)
    region_col = jnp.sum(jnp.where(diag, region_row, 0), axis=1, keepdims=True)
    before = (region_col == region_row) & (iota(square, 0) < iota(square, 1))
    rank_row = jnp.sum(jnp.where(before, 1, 0), axis=0, keepdims=True)
    slot_row = region_row * CAP + rank_row
    place = jnp.where(iota((BOX, TERM), 0) == slot_row, 1.0, 0.0).astype(BF16)

    def spectrum(values, j):
        high, low = two(values)
        return dot(high, table[j, 0]) + (dot(low, table[j, 0]) + dot(high, table[j, 1]))

    def pack(values):
        high, low = two(values)
        return dot(place, high) + dot(place, low)

    def post(j, boxes):
        for c in range(2):
            packed[j, c] = boxes[:, c * HARM : (c + 1) * HARM]

    def item_copy(j, to):
        return pltpu.make_async_remote_copy(
            packed.at[j, :, pl.ds(pl.multiple_of(to * CAP, CAP), CAP), :],
            landed.at[j, :, pl.ds(pl.multiple_of(region * CAP, CAP), CAP), :],
            item_send.at[j],
            item_recv.at[j],
            device_id={"region": to, "sub": sub},
            device_id_type=MESH,
        )

    def own_copy(j):
        own = pl.ds(pl.multiple_of(region * CAP, CAP), CAP)
        return pltpu.make_async_copy(packed.at[j, :, own, :], landed.at[j, :, own, :], own_sem.at[j])

    def send_items(j):
        own_copy(j).start()

        def send(i, _):
            item_copy(j, lax.rem(region + i, REGIONS)).start()
            return 0

        lax.fori_loop(1, REGIONS, send, 0)

    def line_copies(j):
        copies = []
        for at, count, to, device in ((0, 2, 0, other_sub), (2, 1, 3, below), (3, 1, 2, above)):
            copies.append(
                pltpu.make_async_remote_copy(
                    outgo.at[j, pl.ds(at, count)],
                    arrived.at[j, pl.ds(to, count)],
                    line_send.at[j, at],
                    line_recv.at[j, to],
                    device_id=device,
                    device_id_type=MESH,
                )
            )
        return copies

    def put_lines(j, line_volts, rows):
        going = jnp.where(live, twice_admit * line_volts - rows, 0.0)
        outgo[j, 0] = going[LPP : 2 * LPP]
        outgo[j, 1] = going[:LPP]
        outgo[j, 2] = going[2 * LPP : 3 * LPP]
        outgo[j, 3] = going[3 * LPP :]

    head = pl.ds(0, TERM)
    span0 = pl.ds(PAD, COLS)
    span1 = pl.ds(PAD + COLS, COLS)
    term_gain = gain[head, :][:, :1]
    loads[0].wait()
    mat_loads[0].wait()
    part = dot(mat[head, :], rhs[:, pl.ds(0, PAD + COLS)])
    reach = part[:, :PAD] + term_gain * rhs[head, pl.ds(0, PAD)].astype(F32)
    reach_high, reach_low = two(reach)
    term_lane = iota((TERM, LANES), 1)
    reach_parts = jnp.where(
        (term_lane < SLOTS) | ((term_lane >= 2 * SLOTS) & (term_lane < 3 * SLOTS)),
        reach_high.astype(F32),
        jnp.where(term_lane < 2 * SLOTS, reach_low.astype(F32), 0.0),
    ).astype(BF16)
    volts = part[:, PAD:] + term_gain * rhs[head, span0].astype(F32)
    volts = volts + dot(reach_parts, stack4(injected, injected))
    volt_ref[head, pl.ds(0, COLS)] = volts.astype(BF16)
    for load in loads[2:]:
        load.wait()
    base = jnp.concatenate([prior[pl.ds(0, TERM, stride=2), :], prior[pl.ds(1, TERM, stride=2), :]], axis=1)
    fit = base + spectrum(volts - old[:, :COLS].astype(F32), 0)
    post(0, pack(fit))

    for load in mat_loads[1:]:
        load.wait()

    def pick(k, _):
        node = jnp.maximum(nodes_ref[k // LPP, k % LPP], 0)
        group = lax.div(node, 16) * 16
        rows = mat[pl.ds(group, 16), :].astype(F32)
        row = jnp.sum(jnp.where(iota((16, 1), 0) == node - group, rows, 0.0), axis=0, keepdims=True)
        gathered[pl.ds(k, 1), :] = row
        return 0

    lax.fori_loop(0, SLOTS, pick, 0, unroll=4)
    picked[:SLOTS, :] = gathered[...].astype(BF16)
    line_part = dot(picked[...], rhs[:, pl.ds(0, PAD + COLS)])
    line_reach = line_part[:SLOTS, :PAD] + line_gain * jnp.where(same, 1.0, 0.0)
    line_high, line_low = two(line_reach)
    line_parts = jnp.where(
        lane < SLOTS, line_high.astype(F32), jnp.where(lane < 2 * SLOTS, line_low.astype(F32), 0.0)
    ).astype(BF16)
    line_volts = line_part[:SLOTS, PAD:] + line_gain * line_part[SLOTS:, PAD:]
    line_volts = line_volts + dot(line_parts, stack4(injected, injected))
    put_lines(0, line_volts, line_rows)

    pl.semaphore_wait(barrier, REGIONS)
    lines0 = line_copies(0)
    for copy in lines0:
        copy.start()
    send_items(0)

    loads[1].wait()
    fresh[...] = dot(mat[head, :], rhs[:, span1]) + term_gain * rhs[head, span1].astype(F32)
    fit = fit + spectrum(fresh[...] - old[:, COLS:].astype(F32), 1)
    post(1, pack(fit))
    reach_box = dot(place, reach_parts).astype(BF16)
    line_part = dot(picked[...], rhs[:, span1])
    line_base = line_part[:SLOTS] + line_gain * line_part[SLOTS:]

    def inject(columns, rows32):
        block = stack4(rows32)

        def step(i, _):
            rows = pl.ds(pl.multiple_of(i * BLOCK, BLOCK), BLOCK)
            added = dot(rhs[rows, pl.ds(0, PAD)], block)
            rhs[rows, columns] = (rhs[rows, columns].astype(F32) + added).astype(BF16)
            return 0

        lax.fori_loop(0, NODES // BLOCK, step, 0)

    def advance(low, high, first_col, count):
        def step(i, _):
            rows = pl.ds(pl.multiple_of(i * BLOCK, BLOCK), BLOCK)
            columns = pl.ds(PAD + first_col, count)
            total = dot(mat[rows, :], rhs[:, columns])
            total = total + gain[rows, :][:, :1] * rhs[rows, columns].astype(F32)
            volt_ref[rows, pl.ds(first_col, count)] = total.astype(BF16)
            return 0

        lax.fori_loop(low, high, step, 0)

    inject(span0, injected)
    advance(1, 1 + EARLY, 0, SPLIT)

    for copy in lines0:
        copy.wait()
    line_rows = arrived[0].reshape(SLOTS, COLS)
    injected = line_injection(line_rows)
    shift_high, shift_low = two(dot(injected, table[1, 0]) + dot(injected, table[1, 1]))
    boxes = dot(reach_box, stack4(shift_high, shift_high, shift_low))
    for c in range(2):
        packed[1, c] = packed[1, c] + boxes[:, c * HARM : (c + 1) * HARM]
    both = stack4(injected, injected)
    put_lines(1, line_base + dot(line_parts, both), line_rows)
    volt_ref[head, pl.ds(COLS, COLS)] = (fresh[...] + dot(reach_parts, both)).astype(BF16)
    send_items(1)
    lines1 = line_copies(1)
    for copy in lines1:
        copy.start()

    advance(1 + EARLY, NODES // BLOCK, 0, SPLIT)
    inject(span1, injected)
    advance(1, NODES // BLOCK, SPLIT, WIDE - SPLIT)

    for copy in lines1:
        copy.wait()
    next_ref[...] = arrived[1]
    for j in range(SPANS):
        own_copy(j).wait()
        sent = packed.at[j, :, pl.ds(0, BOX - CAP), :]
        pltpu.make_async_copy(sent, sent, item_send.at[j]).wait()
        came = landed.at[j, :, pl.ds(0, BOX - CAP), :]
        pltpu.make_async_copy(came, came, item_recv.at[j]).wait()
        for c in range(2):
            phasor_ref[pl.ds(2 * j + c, BOX, stride=4), :] = landed[j, c]


def body(
    sources,
    coupling,
    self_term,
    history,
    line_nodes,
    line_admit,
    term_region,
    old_samples,
    prior_phasor,
):
    any_space = pl.BlockSpec(memory_space=pl.ANY)
    vmem = pl.BlockSpec(memory_space=pltpu.VMEM)
    smem = pl.BlockSpec(memory_space=pltpu.SMEM)
    volts, phasors, following = pl.pallas_call(
        kernel,
        out_shape=(
            jax.ShapeDtypeStruct((NODES, WIDE), BF16),
            jax.ShapeDtypeStruct((BOX * 2 * SPANS, HARM), F32),
            jax.ShapeDtypeStruct((NEIGH, LPP, COLS), F32),
        ),
        in_specs=[smem, smem] + [any_space] * 5 + [vmem] * 3,
        out_specs=(vmem, vmem, vmem),
        scratch_shapes=[
            pltpu.VMEM((NODES, NODES), BF16),
            pltpu.VMEM((NODES, PAD + WIDE), BF16),
            pltpu.VMEM((TERM, WIDE), BF16),
            pltpu.VMEM((2 * TERM, HARM), F32),
            pltpu.VMEM((SPANS, 2, COLS, 2 * HARM), BF16),
            pltpu.VMEM((NODES, LANES), F32),
            pltpu.VMEM((2 * SLOTS, NODES), BF16),
            pltpu.VMEM((SLOTS, NODES), F32),
            pltpu.VMEM((TERM, COLS), F32),
            pltpu.VMEM((SPANS, NEIGH, LPP, COLS), F32),
            pltpu.VMEM((SPANS, NEIGH, LPP, COLS), F32),
            pltpu.VMEM((SPANS, 2, BOX, HARM), F32),
            pltpu.VMEM((SPANS, 2, BOX, HARM), F32),
            pltpu.SemaphoreType.DMA((NODES // BLOCK,)),
            pltpu.SemaphoreType.DMA((5,)),
            pltpu.SemaphoreType.DMA((SPANS, NEIGH)),
            pltpu.SemaphoreType.DMA((SPANS, NEIGH)),
            pltpu.SemaphoreType.DMA((SPANS,)),
            pltpu.SemaphoreType.DMA((SPANS,)),
            pltpu.SemaphoreType.DMA((SPANS,)),
        ],
        compiler_params=pltpu.CompilerParams(
            collective_id=0, has_side_effects=True, vmem_limit_bytes=56 << 20
        ),
        name="transient",
    )(
        line_nodes[0],
        line_admit[0],
        sources[0],
        coupling[0],
        old_samples,
        prior_phasor.reshape(2 * TERM, HARM),
        jnp.asarray(fit_tables()),
        history.reshape(SLOTS, COLS),
        self_term,
        term_region.reshape(1, TERM),
    )
    return following[None], volts[None], phasors.reshape(BOX, SPANS, 2, HARM)


def solution(mesh):
    return jax.shard_map(
        body,
        mesh=mesh,
        in_specs=(
            P(("region", "sub"), None, None),
            P(("region", "sub"), None, None),
            P(("region", "sub"), None),
            P(("region", "sub"), None, None, None),
            P(("region", "sub"), None, None),
            P(("region", "sub"), None, None),
            P(("region", "sub"), None),
            P(("region", "sub"), None),
            P(("region", "sub"), None, None),
        ),
        out_specs=(
            P(("region", "sub"), None, None, None),
            P(("region", "sub"), None, None),
            P(("region", "sub"), None, None, None),
        ),
        check_vma=False,
    )
```

```python
import math

import jax
import jax.numpy as jnp
import numpy as np
from jax import lax
from jax.experimental import pallas as pl
from jax.experimental.pallas import tpu as pltpu
from jax.sharding import PartitionSpec as P

NODES = 2048
NEIGH = 4
LPP = 8
SLOTS = NEIGH * LPP
DELAY = 40
SPANS = 2
SCEN = 16
TERM = 256
BINS = 8
DFT_LEN = 2048
COLS = DELAY * SCEN
WIDE = SPANS * COLS
REGIONS = 64
CAP = 8
BOX = REGIONS * CAP
LANES = 128
HARM = BINS * SCEN
PAD = 128
BLOCK = 256
LATE = 1
PIECE = 8
FILL = 512
CHUNKS = 8
MESH = pl.DeviceIdType.MESH
F32 = jnp.float32
BF16 = jnp.bfloat16
HELD = (
    ((NODES, WIDE), BF16),
    ((SPANS, 2, BOX, HARM), F32),
    ((SPANS, NEIGH, LPP, COLS), F32),
    ((2 * SLOTS + NODES, NODES), BF16),
    ((NODES, PAD + WIDE), BF16),
    ((NODES, LANES), F32),
)
RESULTS = (
    ((NODES, WIDE), BF16),
    ((BOX * 2 * SPANS, HARM), F32),
    ((NEIGH, LPP, COLS), F32),
)


def far_first():
    away = (0, 1, 2, 1)
    offsets = [(a, b, c, d) for a in range(4) for b in range(4) for c in range(2) for d in range(2)]
    return sorted(offsets[1:], key=lambda o: -(away[o[0]] + away[o[1]] + 2 * o[2]))


def fit_tables():
    step = np.arange(SPANS * DELAY)
    bins = np.arange(1, BINS + 1)
    angle = (step[:, None] * bins[None, :] % DFT_LEN) * (2.0 * math.pi / DFT_LEN)
    wave = np.stack([np.cos(angle), -np.sin(angle)], axis=1) / math.sqrt(DFT_LEN)
    table = np.einsum("uch,st->uscht", wave, np.eye(SCEN))
    table = table.reshape(SPANS, COLS, 2 * HARM).astype(np.float32)
    high = table.astype(BF16)
    low = (table - high.astype(np.float32)).astype(BF16)
    return np.stack([high, low], axis=1)


def dot(a, b):
    return jnp.dot(a, b, preferred_element_type=F32)


def two(x):
    high = x.astype(BF16)
    return high, (x - high.astype(F32)).astype(BF16)


def stack4(*blocks):
    zero = jnp.zeros((SLOTS, blocks[0].shape[1]), BF16)
    blocks = blocks + (zero,) * (4 - len(blocks))
    return jnp.concatenate(blocks, axis=0)


def iota(shape, axis):
    return lax.broadcasted_iota(jnp.int32, shape, axis)


def kernel(
    nodes_ref,
    admit_ref,
    src_hbm,
    mat_hbm,
    old_hbm,
    prior_hbm,
    table_hbm,
    hist_ref,
    self_ref,
    region_ref,
    volt_ref,
    landed,
    arrived,
    mat,
    rhs,
    gain,
    old,
    prior,
    table,
    groups,
    fresh,
    outgo,
    packed,
    mat_sem,
    load_sem,
    line_send,
    line_recv,
    item_send,
    item_recv,
    own_sem,
):
    region = lax.axis_index("region")
    sub = lax.axis_index("sub")
    barrier = pltpu.get_barrier_semaphore()
    other_sub = {"region": region, "sub": 1 - sub}
    below = {"region": lax.rem(region + REGIONS - 1, REGIONS), "sub": sub}
    above = {"region": lax.rem(region + 1, REGIONS), "sub": sub}

    loads = [
        pltpu.make_async_copy(
            src_hbm.at[:, pl.ds(j * COLS, COLS)], rhs.at[:, pl.ds(PAD + j * COLS, COLS)], load_sem.at[j]
        )
        for j in range(SPANS)
    ]
    loads.append(pltpu.make_async_copy(old_hbm, old, load_sem.at[2]))
    loads.append(pltpu.make_async_copy(prior_hbm, prior, load_sem.at[3]))
    for j in range(SPANS):
        loads.append(pltpu.make_async_copy(table_hbm.at[j], table.at[j], load_sem.at[4 + j]))
    mat_loads = [
        pltpu.make_async_copy(
            mat_hbm.at[pl.ds(i * BLOCK, BLOCK)],
            mat.at[pl.ds(2 * SLOTS + i * BLOCK, BLOCK)],
            mat_sem.at[i],
        )
        for i in range(NODES // BLOCK)
    ]
    loads[0].start()
    for load in mat_loads:
        load.start()
    for i in (2, 3, 4, 1, 5):
        loads[i].start()

    z_at, y_at, x_at, core_at = region // 16, region // 4 % 4, region // 2 % 2, region % 2
    z_part = [(z_at + i) % 4 * 16 for i in range(4)]
    y_part = [(y_at + i) % 4 * 4 for i in range(4)]
    x_part = [(x_at + i) % 2 * 2 for i in range(2)]
    core_part = [(core_at + i) % 2 for i in range(2)]
    peers = [z_part[a] + y_part[b] + (x_part[c] + core_part[d]) for a, b, c, d in far_first()]
    for peer in peers:
        pl.semaphore_signal(
            barrier, inc=1, device_id={"region": peer, "sub": sub}, device_id_type=MESH
        )
    pl.semaphore_signal(barrier, inc=1, device_id=other_sub, device_id_type=MESH)

    node_row = jnp.full((1, LANES), -1, jnp.int32)
    node_col = jnp.full((SLOTS, 1), -1, jnp.int32)
    admit_col = jnp.zeros((SLOTS, 1), F32)
    lane_slot = iota((1, LANES), 1) % SLOTS
    slot_id = iota((SLOTS, 1), 0)
    for k in range(SLOTS):
        node = nodes_ref[k // LPP, k % LPP]
        node_row = jnp.where(lane_slot == k, node, node_row)
        node_col = jnp.where(slot_id == k, node, node_col)
        admit_col = jnp.where(slot_id == k, admit_ref[k // LPP, k % LPP], admit_col)
    live = node_col >= 0
    same = (node_col == node_row) & live
    lane = iota((SLOTS, LANES), 1)
    earlier = jnp.where(same & (lane < slot_id), 1.0, 0.0)
    first = (jnp.sum(earlier, axis=1, keepdims=True) == 0.0) & live
    merge = jnp.where(same & (lane < 3 * SLOTS), 1.0, 0.0).astype(BF16)
    twice_admit = 2.0 * admit_col

    def line_injection(rows):
        high = rows.astype(BF16)
        rest = rows - high.astype(F32)
        mid = rest.astype(BF16)
        low = (rest - mid.astype(F32)).astype(BF16)
        total = dot(merge, stack4(high, mid, low))
        return jnp.where(first, total, 0.0).astype(BF16)

    def mark(i, _):
        rows = pl.ds(pl.multiple_of(i * BLOCK, BLOCK), BLOCK)
        number = iota((BLOCK, LANES), 0) + i * BLOCK
        rhs[rows, pl.ds(0, PAD)] = jnp.where(number == node_row, 1.0, 0.0).astype(BF16)
        return 0

    def weigh(i, _):
        rows = pl.ds(pl.multiple_of(i * BLOCK, BLOCK), BLOCK)
        diag = iota((BLOCK, BLOCK), 0) == iota((BLOCK, BLOCK), 1)
        gains = jnp.sum(jnp.where(diag, self_ref[:, rows], 0.0), axis=1, keepdims=True)
        gain[rows, :] = jnp.broadcast_to(gains, (BLOCK, LANES))
        return 0

    lax.fori_loop(0, NODES // BLOCK, mark, 0)
    weigh(0, 0)
    line_rows = hist_ref[...]
    injected = line_injection(line_rows)

    region_row = region_ref[...]
    square = (TERM, TERM)
    diag = iota(square, 0) == iota(square, 1)
    region_col = jnp.sum(jnp.where(diag, region_row, 0), axis=1, keepdims=True)
    before = (region_col == region_row) & (iota(square, 0) < iota(square, 1))
    rank_row = jnp.sum(jnp.where(before, 1, 0), axis=0, keepdims=True)
    slot_row = region_row * CAP + rank_row
    place = jnp.where(iota((BOX, TERM), 0) == slot_row, 1.0, 0.0).astype(BF16)

    def spectrum(values, j):
        high, low = two(values)
        return dot(high, table[j, 0]) + (dot(low, table[j, 0]) + dot(high, table[j, 1]))

    def pack(values):
        high, low = two(values)
        return dot(place, high) + dot(place, low)

    def post(j, boxes):
        for c in range(2):
            packed[j, c] = boxes[:, c * HARM : (c + 1) * HARM]

    def item_copy(j, to):
        return pltpu.make_async_remote_copy(
            packed.at[j, :, pl.ds(pl.multiple_of(to * CAP, CAP), CAP), :],
            landed.at[j, :, pl.ds(pl.multiple_of(region * CAP, CAP), CAP), :],
            item_send.at[j],
            item_recv.at[j],
            device_id={"region": to, "sub": sub},
            device_id_type=MESH,
        )

    def own_copy(j):
        own = pl.ds(pl.multiple_of(region * CAP, CAP), CAP)
        return pltpu.make_async_copy(packed.at[j, :, own, :], landed.at[j, :, own, :], own_sem.at[j])

    def send_items(j, some):
        for peer in some:
            item_copy(j, peer).start()

    def line_copies(j):
        copies = []
        for at, count, to, device in ((0, 2, 0, other_sub), (2, 1, 3, below), (3, 1, 2, above)):
            copies.append(
                pltpu.make_async_remote_copy(
                    outgo.at[j, pl.ds(at, count)],
                    arrived.at[j, pl.ds(to, count)],
                    line_send.at[j, at],
                    line_recv.at[j, to],
                    device_id=device,
                    device_id_type=MESH,
                )
            )
        return copies

    def put_lines(j, line_volts, rows):
        going = jnp.where(live, twice_admit * line_volts - rows, 0.0)
        outgo[j, 0] = going[LPP : 2 * LPP]
        outgo[j, 1] = going[:LPP]
        outgo[j, 2] = going[2 * LPP : 3 * LPP]
        outgo[j, 3] = going[3 * LPP :]

    head = pl.ds(0, TERM)
    span0 = pl.ds(PAD, COLS)
    span1 = pl.ds(PAD + COLS, COLS)
    term_gain = gain[head, :][:, :1]
    loads[0].wait()
    mat_loads[0].wait()
    part = dot(mat[pl.ds(2 * SLOTS, TERM), :], rhs[:, pl.ds(0, PAD + COLS)])
    reach = part[:, :PAD] + term_gain * rhs[head, pl.ds(0, PAD)].astype(F32)
    reach_high, reach_low = two(reach)
    term_lane = iota((TERM, LANES), 1)
    reach_parts = jnp.where(
        (term_lane < SLOTS) | ((term_lane >= 2 * SLOTS) & (term_lane < 3 * SLOTS)),
        reach_high.astype(F32),
        jnp.where(term_lane < 2 * SLOTS, reach_low.astype(F32), 0.0),
    ).astype(BF16)
    volts = part[:, PAD:] + term_gain * rhs[head, span0].astype(F32)
    fresh[0] = volts + dot(reach_parts, stack4(injected, injected))

    lax.fori_loop(1, NODES // BLOCK, weigh, 0)
    chosen = jnp.where(node_col == iota((SLOTS, NODES), 1), 1.0, 0.0)
    line_gain = jnp.sum(chosen * self_ref[...], axis=1, keepdims=True)
    mat[SLOTS : 2 * SLOTS, :] = chosen.astype(BF16)
    node_at = jnp.maximum(node_col, 0) % PIECE + slot_id * PIECE
    choice = jnp.where(iota((SLOTS, SLOTS * PIECE), 1) == node_at, 1.0, 0.0).astype(BF16)
    for load in mat_loads[1:]:
        load.wait()
    for k in range(SLOTS):
        node = jnp.maximum(nodes_ref[k // LPP, k % LPP], 0)
        group = 2 * SLOTS + lax.div(node, PIECE) * PIECE
        groups[k * PIECE : (k + 1) * PIECE, :] = mat[pl.ds(group, PIECE), :]
    mat[:SLOTS, :] = dot(choice, groups[...]).astype(BF16)
    line_part = dot(mat[: 2 * SLOTS, :], rhs[:, pl.ds(0, PAD + COLS)])
    line_reach = line_part[:SLOTS, :PAD] + line_gain * jnp.where(same, 1.0, 0.0)
    line_high, line_low = two(line_reach)
    line_parts = jnp.where(
        lane < SLOTS, line_high.astype(F32), jnp.where(lane < 2 * SLOTS, line_low.astype(F32), 0.0)
    ).astype(BF16)
    line_volts = line_part[:SLOTS, PAD:] + line_gain * line_part[SLOTS:, PAD:]
    line_volts = line_volts + dot(line_parts, stack4(injected, injected))
    put_lines(0, line_volts, line_rows)

    pl.semaphore_wait(barrier, REGIONS)
    lines0 = line_copies(0)
    for copy in lines0:
        copy.start()

    for load in loads[2:5]:
        load.wait()
    base = jnp.concatenate([prior[pl.ds(0, TERM, stride=2), :], prior[pl.ds(1, TERM, stride=2), :]], axis=1)
    fit = base + spectrum(fresh[0] - old[:, :COLS].astype(F32), 0)
    post(0, pack(fit))
    send_items(0, peers)
    own_copy(0).start()
    volt_ref[head, pl.ds(0, COLS)] = fresh[0].astype(BF16)

    loads[1].wait()
    loads[5].wait()
    part = dot(mat[: 2 * SLOTS + TERM, :], rhs[:, span1])
    line_base = part[:SLOTS] + line_gain * part[SLOTS : 2 * SLOTS]
    fresh[1] = part[2 * SLOTS :] + term_gain * rhs[head, span1].astype(F32)
    fit = fit + spectrum(fresh[1] - old[:, COLS:].astype(F32), 1)
    post(1, pack(fit))
    reach_box = dot(place, reach_parts).astype(BF16)

    for copy in lines0:
        copy.wait()
    line_rows = arrived[0].reshape(SLOTS, COLS)
    late = line_injection(line_rows)
    shift_high, shift_low = two(dot(late, table[1, 0]) + dot(late, table[1, 1]))
    boxes = dot(reach_box, stack4(shift_high, shift_high, shift_low))
    for c in range(2):
        packed[1, c] = packed[1, c] + boxes[:, c * HARM : (c + 1) * HARM]
    send_items(1, peers)
    own_copy(1).start()
    both = stack4(late, late)
    put_lines(1, line_base + dot(line_parts, both), line_rows)
    volt_ref[head, pl.ds(COLS, COLS)] = (fresh[1] + dot(reach_parts, both)).astype(BF16)
    lines1 = line_copies(1)
    for copy in lines1:
        copy.start()

    injection = stack4(jnp.concatenate([injected, late], axis=1))

    def inject(i, _):
        rows = pl.ds(pl.multiple_of(i * FILL, FILL), FILL)
        columns = pl.ds(PAD, WIDE)
        added = dot(rhs[rows, pl.ds(0, PAD)], injection)
        rhs[rows, columns] = (rhs[rows, columns].astype(F32) + added).astype(BF16)
        return 0

    lax.fori_loop(0, NODES // FILL, inject, 0)

    def advance(i, _):
        rows = pl.ds(pl.multiple_of(i * BLOCK, BLOCK), BLOCK)
        total = dot(mat[pl.ds(2 * SLOTS + i * BLOCK, BLOCK), :], rhs[:, pl.ds(PAD, WIDE)])
        total = total + gain[rows, :][:, :1] * rhs[rows, pl.ds(PAD, WIDE)].astype(F32)
        volt_ref[rows, :] = total.astype(BF16)
        return 0

    lax.fori_loop(1, NODES // BLOCK - LATE, advance, 0)

    for copy in lines1:
        copy.wait()
    for j in range(SPANS):
        own_copy(j).wait()
        sent = packed.at[j, :, pl.ds(0, BOX - CAP), :]
        pltpu.make_async_copy(sent, sent, item_send.at[j]).wait()
        came = landed.at[j, :, pl.ds(0, BOX - CAP), :]
        pltpu.make_async_copy(came, came, item_recv.at[j]).wait()


def release(
    volt_ref, landed, arrived, mat, rhs, gain, volt_hbm, phasor_hbm, next_hbm, phasors, last, sem
):
    done = NODES - LATE * BLOCK
    rows = done // CHUNKS
    copies = [
        pltpu.make_async_copy(
            volt_ref.at[pl.ds(i * rows, rows)], volt_hbm.at[pl.ds(i * rows, rows)], sem.at[i]
        )
        for i in range(CHUNKS)
    ]
    copies.append(pltpu.make_async_copy(arrived.at[SPANS - 1], next_hbm, sem.at[CHUNKS]))
    for copy in copies:
        copy.start()
    for j in range(SPANS):
        for c in range(2):
            phasors[pl.ds(2 * j + c, BOX, stride=2 * SPANS), :] = landed[j, c]
    copies.append(pltpu.make_async_copy(phasors, phasor_hbm, sem.at[CHUNKS + 1]))
    copies[-1].start()
    for i in range(LATE):
        low = done + i * BLOCK
        total = dot(mat[2 * SLOTS + low : 2 * SLOTS + low + BLOCK, :], rhs[:, PAD:])
        total = total + gain[low : low + BLOCK, :][:, :1] * rhs[low : low + BLOCK, PAD:].astype(F32)
        last[i * BLOCK : (i + 1) * BLOCK, :] = total.astype(BF16)
        copies.append(
            pltpu.make_async_copy(
                last.at[pl.ds(i * BLOCK, BLOCK)], volt_hbm.at[pl.ds(low, BLOCK)], sem.at[CHUNKS + 2 + i]
            )
        )
        copies[-1].start()
    for copy in copies:
        copy.wait()


def body(
    sources,
    coupling,
    self_term,
    history,
    line_nodes,
    line_admit,
    term_region,
    old_samples,
    prior_phasor,
):
    any_space = pl.BlockSpec(memory_space=pl.ANY)
    hbm = pl.BlockSpec(memory_space=pltpu.HBM)
    vmem = pl.BlockSpec(memory_space=pltpu.VMEM)
    smem = pl.BlockSpec(memory_space=pltpu.SMEM)
    held = pl.pallas_call(
        kernel,
        out_shape=tuple(pltpu.VMEM(shape, dtype) for shape, dtype in HELD),
        in_specs=[smem, smem] + [hbm] * 5 + [vmem] * 3,
        out_specs=(vmem,) * len(HELD),
        scratch_shapes=[
            pltpu.VMEM((TERM, WIDE), BF16),
            pltpu.VMEM((2 * TERM, HARM), F32),
            pltpu.VMEM((SPANS, 2, COLS, 2 * HARM), BF16),
            pltpu.VMEM((SLOTS * PIECE, NODES), BF16),
            pltpu.VMEM((SPANS, TERM, COLS), F32),
            pltpu.VMEM((SPANS, NEIGH, LPP, COLS), F32),
            pltpu.VMEM((SPANS, 2, BOX, HARM), F32),
            pltpu.SemaphoreType.DMA((NODES // BLOCK,)),
            pltpu.SemaphoreType.DMA((6,)),
            pltpu.SemaphoreType.DMA((SPANS, NEIGH)),
            pltpu.SemaphoreType.DMA((SPANS, NEIGH)),
            pltpu.SemaphoreType.DMA((SPANS,)),
            pltpu.SemaphoreType.DMA((SPANS,)),
            pltpu.SemaphoreType.DMA((SPANS,)),
        ],
        compiler_params=pltpu.CompilerParams(
            collective_id=0, has_side_effects=True, vmem_limit_bytes=38 << 20
        ),
        name="transient",
    )(
        line_nodes[0],
        line_admit[0],
        sources[0],
        coupling[0],
        old_samples,
        prior_phasor.reshape(2 * TERM, HARM),
        jnp.asarray(fit_tables()),
        history.reshape(SLOTS, COLS),
        self_term,
        term_region.reshape(1, TERM),
    )
    volts, phasors, following = pl.pallas_call(
        release,
        out_shape=tuple(jax.ShapeDtypeStruct(shape, dtype) for shape, dtype in RESULTS),
        in_specs=[vmem] * len(HELD),
        out_specs=(any_space,) * 3,
        scratch_shapes=[
            pltpu.VMEM((BOX * 2 * SPANS, HARM), F32),
            pltpu.VMEM((LATE * BLOCK, WIDE), BF16),
            pltpu.SemaphoreType.DMA((CHUNKS + 2 + LATE,)),
        ],
        compiler_params=pltpu.CompilerParams(vmem_limit_bytes=6 << 20),
        name="release",
    )(*held)
    return following[None], volts[None], phasors.reshape(BOX, SPANS, 2, HARM)


def solution(mesh):
    return jax.shard_map(
        body,
        mesh=mesh,
        in_specs=(
            P(("region", "sub"), None, None),
            P(("region", "sub"), None, None),
            P(("region", "sub"), None),
            P(("region", "sub"), None, None, None),
            P(("region", "sub"), None, None),
            P(("region", "sub"), None, None),
            P(("region", "sub"), None),
            P(("region", "sub"), None),
            P(("region", "sub"), None, None),
        ),
        out_specs=(
            P(("region", "sub"), None, None, None),
            P(("region", "sub"), None, None),
            P(("region", "sub"), None, None, None),
        ),
        check_vma=False,
    )
```

```python
import math

import jax
import jax.numpy as jnp
import numpy as np
from jax import lax
from jax.experimental import pallas as pl
from jax.experimental.pallas import tpu as pltpu
from jax.sharding import PartitionSpec as P

NODES = 2048
NEIGH = 4
LPP = 8
SLOTS = NEIGH * LPP
DELAY = 40
SPANS = 2
SCEN = 16
TERM = 256
BINS = 8
DFT_LEN = 2048
COLS = DELAY * SCEN
WIDE = SPANS * COLS
REGIONS = 64
CAP = 8
BOX = REGIONS * CAP
LANES = 128
HARM = BINS * SCEN
PAD = 128
BLOCK = 256
LATE = 1
PIECE = 8
FILL = 1024
CHUNKS = 8
MESH = pl.DeviceIdType.MESH
F32 = jnp.float32
BF16 = jnp.bfloat16
HELD = (
    ((NODES, WIDE), BF16),
    ((SPANS, 2, BOX, HARM), F32),
    ((SPANS, NEIGH, LPP, COLS), F32),
    ((2 * SLOTS + NODES, NODES), BF16),
    ((NODES, PAD + WIDE), BF16),
    ((NODES, LANES), F32),
)
RESULTS = (
    ((NODES, WIDE), BF16),
    ((BOX * 2 * SPANS, HARM), F32),
    ((NEIGH, LPP, COLS), F32),
)


def far_first():
    away = (0, 1, 2, 1)
    offsets = [(a, b, c, d) for a in range(4) for b in range(4) for c in range(2) for d in range(2)]
    return sorted(offsets[1:], key=lambda o: -(away[o[0]] + away[o[1]] + 2 * o[2]))


def fit_tables():
    step = np.arange(SPANS * DELAY)
    bins = np.arange(1, BINS + 1)
    angle = (step[:, None] * bins[None, :] % DFT_LEN) * (2.0 * math.pi / DFT_LEN)
    wave = np.stack([np.cos(angle), -np.sin(angle)], axis=1) / math.sqrt(DFT_LEN)
    table = np.einsum("uch,st->uscht", wave, np.eye(SCEN))
    table = table.reshape(SPANS, COLS, 2 * HARM).astype(np.float32)
    high = table.astype(BF16)
    low = (table - high.astype(np.float32)).astype(BF16)
    return np.stack([high, low], axis=1)


def dot(a, b):
    return jnp.dot(a, b, preferred_element_type=F32)


def two(x):
    high = x.astype(BF16)
    return high, (x - high.astype(F32)).astype(BF16)


def stack4(*blocks):
    zero = jnp.zeros((SLOTS, blocks[0].shape[1]), BF16)
    blocks = blocks + (zero,) * (4 - len(blocks))
    return jnp.concatenate(blocks, axis=0)


def iota(shape, axis):
    return lax.broadcasted_iota(jnp.int32, shape, axis)


def kernel(
    nodes_hbm,
    admit_hbm,
    src_hbm,
    mat_hbm,
    old_hbm,
    prior_hbm,
    table_hbm,
    hist_hbm,
    self_hbm,
    region_hbm,
    volt_ref,
    landed,
    arrived,
    mat,
    rhs,
    gain,
    old,
    prior,
    table,
    groups,
    fresh,
    outgo,
    packed,
    mat_sem,
    load_sem,
    line_send,
    line_recv,
    item_send,
    item_recv,
    own_sem,
    nodes_ref,
    admit_ref,
    hist_ref,
    self_ref,
    region_ref,
    small_sem,
):
    region = lax.axis_index("region")
    sub = lax.axis_index("sub")
    barrier = pltpu.get_barrier_semaphore()
    other_sub = {"region": region, "sub": 1 - sub}
    below = {"region": lax.rem(region + REGIONS - 1, REGIONS), "sub": sub}
    above = {"region": lax.rem(region + 1, REGIONS), "sub": sub}

    loads = [
        pltpu.make_async_copy(
            src_hbm.at[:, pl.ds(j * COLS, COLS)], rhs.at[:, pl.ds(PAD + j * COLS, COLS)], load_sem.at[j]
        )
        for j in range(SPANS)
    ]
    loads.append(pltpu.make_async_copy(old_hbm.at[:, :COLS], old.at[:, :COLS], load_sem.at[2]))
    loads.append(pltpu.make_async_copy(prior_hbm, prior, load_sem.at[3]))
    for j in range(SPANS):
        loads.append(pltpu.make_async_copy(table_hbm.at[j], table.at[j], load_sem.at[4 + j]))
    loads.append(pltpu.make_async_copy(old_hbm.at[:, COLS:], old.at[:, COLS:], load_sem.at[6]))
    mat_loads = [
        pltpu.make_async_copy(
            mat_hbm.at[pl.ds(i * BLOCK, BLOCK)],
            mat.at[pl.ds(2 * SLOTS + i * BLOCK, BLOCK)],
            mat_sem.at[i],
        )
        for i in range(NODES // BLOCK)
    ]
    small = [
        pltpu.make_async_copy(*pair, small_sem.at[i])
        for i, pair in enumerate(
            (
                (nodes_hbm, nodes_ref),
                (admit_hbm, admit_ref),
                (hist_hbm, hist_ref),
                (self_hbm, self_ref),
                (region_hbm, region_ref),
            )
        )
    ]
    for load in small:
        load.start()
    loads[0].start()
    mat_loads[0].start()

    z_at, y_at, x_at, core_at = region // 16, region // 4 % 4, region // 2 % 2, region % 2
    z_part = [(z_at + i) % 4 * 16 for i in range(4)]
    y_part = [(y_at + i) % 4 * 4 for i in range(4)]
    x_part = [(x_at + i) % 2 * 2 for i in range(2)]
    core_part = [(core_at + i) % 2 for i in range(2)]
    peers = [z_part[a] + y_part[b] + (x_part[c] + core_part[d]) for a, b, c, d in far_first()]
    for peer in peers:
        pl.semaphore_signal(
            barrier, inc=1, device_id={"region": peer, "sub": sub}, device_id_type=MESH
        )
    pl.semaphore_signal(barrier, inc=1, device_id=other_sub, device_id_type=MESH)

    for load in small:
        load.wait()
    for i in (4, 2, 3):
        loads[i].start()
    for load in mat_loads[1:]:
        load.start()
    for i in (1, 6, 5):
        loads[i].start()

    node_row = jnp.full((1, LANES), -1, jnp.int32)
    node_col = jnp.full((SLOTS, 1), -1, jnp.int32)
    admit_col = jnp.zeros((SLOTS, 1), F32)
    lane_slot = iota((1, LANES), 1) % SLOTS
    slot_id = iota((SLOTS, 1), 0)
    for k in range(SLOTS):
        node = nodes_ref[k // LPP, k % LPP]
        node_row = jnp.where(lane_slot == k, node, node_row)
        node_col = jnp.where(slot_id == k, node, node_col)
        admit_col = jnp.where(slot_id == k, admit_ref[k // LPP, k % LPP], admit_col)
    live = node_col >= 0
    same = (node_col == node_row) & live
    lane = iota((SLOTS, LANES), 1)
    earlier = jnp.where(same & (lane < slot_id), 1.0, 0.0)
    first = (jnp.sum(earlier, axis=1, keepdims=True) == 0.0) & live
    merge = jnp.where(same & (lane < 3 * SLOTS), 1.0, 0.0).astype(BF16)
    twice_admit = 2.0 * admit_col

    def line_injection(rows):
        high = rows.astype(BF16)
        rest = rows - high.astype(F32)
        mid = rest.astype(BF16)
        low = (rest - mid.astype(F32)).astype(BF16)
        total = dot(merge, stack4(high, mid, low))
        return jnp.where(first, total, 0.0).astype(BF16)

    def mark(i, _):
        rows = pl.ds(pl.multiple_of(i * BLOCK, BLOCK), BLOCK)
        number = iota((BLOCK, LANES), 0) + i * BLOCK
        rhs[rows, pl.ds(0, PAD)] = jnp.where(number == node_row, 1.0, 0.0).astype(BF16)
        return 0

    def weigh(i, _):
        rows = pl.ds(pl.multiple_of(i * BLOCK, BLOCK), BLOCK)
        diag = iota((BLOCK, BLOCK), 0) == iota((BLOCK, BLOCK), 1)
        gains = jnp.sum(jnp.where(diag, self_ref[:, rows], 0.0), axis=1, keepdims=True)
        gain[rows, :] = jnp.broadcast_to(gains, (BLOCK, LANES))
        return 0

    lax.fori_loop(0, NODES // BLOCK, mark, 0)
    weigh(0, 0)
    line_rows = hist_ref[...]
    injected = line_injection(line_rows)

    region_row = region_ref[...]
    square = (TERM, TERM)
    diag = iota(square, 0) == iota(square, 1)
    region_col = jnp.sum(jnp.where(diag, region_row, 0), axis=1, keepdims=True)
    before = (region_col == region_row) & (iota(square, 0) < iota(square, 1))
    rank_row = jnp.sum(jnp.where(before, 1, 0), axis=0, keepdims=True)
    slot_row = region_row * CAP + rank_row
    place = jnp.where(iota((BOX, TERM), 0) == slot_row, 1.0, 0.0).astype(BF16)

    def spectrum(values, j):
        high, low = two(values)
        return dot(high, table[j, 0]) + (dot(low, table[j, 0]) + dot(high, table[j, 1]))

    def pack(values):
        high, low = two(values)
        return dot(place, high) + dot(place, low)

    def post(j, boxes):
        for c in range(2):
            packed[j, c] = boxes[:, c * HARM : (c + 1) * HARM]

    def item_copy(j, to):
        return pltpu.make_async_remote_copy(
            packed.at[j, :, pl.ds(pl.multiple_of(to * CAP, CAP), CAP), :],
            landed.at[j, :, pl.ds(pl.multiple_of(region * CAP, CAP), CAP), :],
            item_send.at[j],
            item_recv.at[j],
            device_id={"region": to, "sub": sub},
            device_id_type=MESH,
        )

    def own_copy(j):
        own = pl.ds(pl.multiple_of(region * CAP, CAP), CAP)
        return pltpu.make_async_copy(packed.at[j, :, own, :], landed.at[j, :, own, :], own_sem.at[j])

    def send_items(j, some):
        for peer in some:
            item_copy(j, peer).start()

    def line_copies(j):
        copies = []
        for at, to, device in ((sub, sub, other_sub), (2, 3, below), (3, 2, above)):
            copies.append(
                pltpu.make_async_remote_copy(
                    outgo.at[j, at],
                    arrived.at[j, to],
                    line_send.at[j, len(copies)],
                    line_recv.at[j, len(copies)],
                    device_id=device,
                    device_id_type=MESH,
                )
            )
        return copies

    def put_lines(j, line_volts, rows):
        going = jnp.where(live, twice_admit * line_volts - rows, 0.0)
        outgo[j, 0] = going[LPP : 2 * LPP]
        outgo[j, 1] = going[:LPP]
        outgo[j, 2] = going[2 * LPP : 3 * LPP]
        outgo[j, 3] = going[3 * LPP :]

    head = pl.ds(0, TERM)
    span0 = pl.ds(PAD, COLS)
    span1 = pl.ds(PAD + COLS, COLS)
    term_gain = gain[head, :][:, :1]
    loads[0].wait()
    mat_loads[0].wait()
    part = dot(mat[pl.ds(2 * SLOTS, TERM), :], rhs[:, pl.ds(0, PAD + COLS)])
    reach = part[:, :PAD] + term_gain * rhs[head, pl.ds(0, PAD)].astype(F32)
    reach_high, reach_low = two(reach)
    term_lane = iota((TERM, LANES), 1)
    reach_parts = jnp.where(
        (term_lane < SLOTS) | ((term_lane >= 2 * SLOTS) & (term_lane < 3 * SLOTS)),
        reach_high.astype(F32),
        jnp.where(term_lane < 2 * SLOTS, reach_low.astype(F32), 0.0),
    ).astype(BF16)
    volts = part[:, PAD:] + term_gain * rhs[head, span0].astype(F32)
    fresh[0] = volts + dot(reach_parts, stack4(injected, injected))

    for load in loads[2:5]:
        load.wait()
    base = jnp.concatenate([prior[pl.ds(0, TERM, stride=2), :], prior[pl.ds(1, TERM, stride=2), :]], axis=1)
    fit = base + spectrum(fresh[0] - old[:, :COLS].astype(F32), 0)
    post(0, pack(fit))

    for j in range(SPANS):
        arrived[j, sub] = jnp.zeros((LPP, COLS), F32)
    lax.fori_loop(1, NODES // BLOCK, weigh, 0)
    chosen = jnp.where(node_col == iota((SLOTS, NODES), 1), 1.0, 0.0)
    line_gain = jnp.sum(chosen * self_ref[...], axis=1, keepdims=True)
    mat[SLOTS : 2 * SLOTS, :] = chosen.astype(BF16)
    node_at = jnp.maximum(node_col, 0) % PIECE + slot_id * PIECE
    choice = jnp.where(iota((SLOTS, SLOTS * PIECE), 1) == node_at, 1.0, 0.0).astype(BF16)
    for load in mat_loads[1:]:
        load.wait()
    for k in range(SLOTS):
        node = jnp.maximum(nodes_ref[k // LPP, k % LPP], 0)
        group = 2 * SLOTS + lax.div(node, PIECE) * PIECE
        groups[k * PIECE : (k + 1) * PIECE, :] = mat[pl.ds(group, PIECE), :]
    mat[:SLOTS, :] = dot(choice, groups[...]).astype(BF16)
    line_part = dot(mat[: 2 * SLOTS, :], rhs[:, pl.ds(0, PAD + COLS)])
    line_reach = line_part[:SLOTS, :PAD] + line_gain * jnp.where(same, 1.0, 0.0)
    line_high, line_low = two(line_reach)
    line_parts = jnp.where(
        lane < SLOTS, line_high.astype(F32), jnp.where(lane < 2 * SLOTS, line_low.astype(F32), 0.0)
    ).astype(BF16)
    line_volts = line_part[:SLOTS, PAD:] + line_gain * line_part[SLOTS:, PAD:]
    line_volts = line_volts + dot(line_parts, stack4(injected, injected))
    put_lines(0, line_volts, line_rows)

    pl.semaphore_wait(barrier, REGIONS)
    lines0 = line_copies(0)
    for copy in lines0:
        copy.start()

    send_items(0, peers)
    own_copy(0).start()
    volt_ref[head, pl.ds(0, COLS)] = fresh[0].astype(BF16)

    loads[1].wait()
    loads[5].wait()
    loads[6].wait()
    part = dot(mat[: 2 * SLOTS + TERM, :], rhs[:, span1])
    line_base = part[:SLOTS] + line_gain * part[SLOTS : 2 * SLOTS]
    fresh[1] = part[2 * SLOTS :] + term_gain * rhs[head, span1].astype(F32)
    fit = fit + spectrum(fresh[1] - old[:, COLS:].astype(F32), 1)
    post(1, pack(fit))
    reach_box = dot(place, reach_parts).astype(BF16)

    def inject(j, rows32):
        injection = stack4(rows32)
        columns = pl.ds(PAD + j * COLS, COLS)

        def step(i, _):
            rows = pl.ds(pl.multiple_of(i * FILL, FILL), FILL)
            added = dot(rhs[rows, pl.ds(0, PAD)], injection)
            rhs[rows, columns] = (rhs[rows, columns].astype(F32) + added).astype(BF16)
            return 0

        lax.fori_loop(0, NODES // FILL, step, 0)

    def advance(i, _):
        rows = pl.ds(pl.multiple_of(i * BLOCK, BLOCK), BLOCK)
        total = dot(mat[pl.ds(2 * SLOTS + i * BLOCK, BLOCK), :], rhs[:, pl.ds(PAD, WIDE)])
        total = total + gain[rows, :][:, :1] * rhs[rows, pl.ds(PAD, WIDE)].astype(F32)
        volt_ref[rows, :] = total.astype(BF16)
        return 0

    inject(0, injected)

    for copy in lines0:
        copy.wait()
    line_rows = arrived[0].reshape(SLOTS, COLS)
    late = line_injection(line_rows)
    shift_high, shift_low = two(dot(late, table[1, 0]) + dot(late, table[1, 1]))
    boxes = dot(reach_box, stack4(shift_high, shift_high, shift_low))
    for c in range(2):
        packed[1, c] = packed[1, c] + boxes[:, c * HARM : (c + 1) * HARM]
    send_items(1, peers)
    own_copy(1).start()
    both = stack4(late, late)
    put_lines(1, line_base + dot(line_parts, both), line_rows)
    volt_ref[head, pl.ds(COLS, COLS)] = (fresh[1] + dot(reach_parts, both)).astype(BF16)
    lines1 = line_copies(1)
    for copy in lines1:
        copy.start()

    inject(1, late)
    lax.fori_loop(1, NODES // BLOCK - LATE, advance, 0)

    for copy in lines1:
        copy.wait()
    for j in range(SPANS):
        own_copy(j).wait()
        sent = packed.at[j, :, pl.ds(0, BOX - CAP), :]
        pltpu.make_async_copy(sent, sent, item_send.at[j]).wait()
        came = landed.at[j, :, pl.ds(0, BOX - CAP), :]
        pltpu.make_async_copy(came, came, item_recv.at[j]).wait()


def release(
    volt_ref, landed, arrived, mat, rhs, gain, volt_hbm, phasor_hbm, next_hbm, phasors, last, sem
):
    done = NODES - LATE * BLOCK
    rows = done // CHUNKS
    copies = [
        pltpu.make_async_copy(
            volt_ref.at[pl.ds(i * rows, rows)], volt_hbm.at[pl.ds(i * rows, rows)], sem.at[i]
        )
        for i in range(CHUNKS)
    ]
    copies.append(pltpu.make_async_copy(arrived.at[SPANS - 1], next_hbm, sem.at[CHUNKS]))
    for copy in copies:
        copy.start()
    for j in range(SPANS):
        for c in range(2):
            phasors[pl.ds(2 * j + c, BOX, stride=2 * SPANS), :] = landed[j, c]
    copies.append(pltpu.make_async_copy(phasors, phasor_hbm, sem.at[CHUNKS + 1]))
    copies[-1].start()
    for i in range(LATE):
        low = done + i * BLOCK
        total = dot(mat[2 * SLOTS + low : 2 * SLOTS + low + BLOCK, :], rhs[:, PAD:])
        total = total + gain[low : low + BLOCK, :][:, :1] * rhs[low : low + BLOCK, PAD:].astype(F32)
        last[i * BLOCK : (i + 1) * BLOCK, :] = total.astype(BF16)
        copies.append(
            pltpu.make_async_copy(
                last.at[pl.ds(i * BLOCK, BLOCK)], volt_hbm.at[pl.ds(low, BLOCK)], sem.at[CHUNKS + 2 + i]
            )
        )
        copies[-1].start()
    for copy in copies:
        copy.wait()


def body(
    sources,
    coupling,
    self_term,
    history,
    line_nodes,
    line_admit,
    term_region,
    old_samples,
    prior_phasor,
):
    any_space = pl.BlockSpec(memory_space=pl.ANY)
    hbm = pl.BlockSpec(memory_space=pltpu.HBM)
    vmem = pl.BlockSpec(memory_space=pltpu.VMEM)
    held = pl.pallas_call(
        kernel,
        out_shape=tuple(pltpu.VMEM(shape, dtype) for shape, dtype in HELD),
        in_specs=[hbm] * 10,
        out_specs=(vmem,) * len(HELD),
        scratch_shapes=[
            pltpu.VMEM((TERM, WIDE), BF16),
            pltpu.VMEM((2 * TERM, HARM), F32),
            pltpu.VMEM((SPANS, 2, COLS, 2 * HARM), BF16),
            pltpu.VMEM((SLOTS * PIECE, NODES), BF16),
            pltpu.VMEM((SPANS, TERM, COLS), F32),
            pltpu.VMEM((SPANS, NEIGH, LPP, COLS), F32),
            pltpu.VMEM((SPANS, 2, BOX, HARM), F32),
            pltpu.SemaphoreType.DMA((NODES // BLOCK,)),
            pltpu.SemaphoreType.DMA((7,)),
            pltpu.SemaphoreType.DMA((SPANS, 3)),
            pltpu.SemaphoreType.DMA((SPANS, 3)),
            pltpu.SemaphoreType.DMA((SPANS,)),
            pltpu.SemaphoreType.DMA((SPANS,)),
            pltpu.SemaphoreType.DMA((SPANS,)),
            pltpu.SMEM((NEIGH, LPP), jnp.int32),
            pltpu.SMEM((NEIGH, LPP), F32),
            pltpu.VMEM((SLOTS, COLS), F32),
            pltpu.VMEM((1, NODES), F32),
            pltpu.VMEM((1, TERM), jnp.int32),
            pltpu.SemaphoreType.DMA((5,)),
        ],
        compiler_params=pltpu.CompilerParams(
            collective_id=0, has_side_effects=True, vmem_limit_bytes=38 << 20
        ),
        name="transient",
    )(
        line_nodes[0],
        line_admit[0],
        sources[0],
        coupling[0],
        old_samples,
        prior_phasor.reshape(2 * TERM, HARM),
        jnp.asarray(fit_tables()),
        history.reshape(SLOTS, COLS),
        self_term,
        term_region.reshape(1, TERM),
    )
    volts, phasors, following = pl.pallas_call(
        release,
        out_shape=tuple(jax.ShapeDtypeStruct(shape, dtype) for shape, dtype in RESULTS),
        in_specs=[vmem] * len(HELD),
        out_specs=(any_space,) * 3,
        scratch_shapes=[
            pltpu.VMEM((BOX * 2 * SPANS, HARM), F32),
            pltpu.VMEM((LATE * BLOCK, WIDE), BF16),
            pltpu.SemaphoreType.DMA((CHUNKS + 2 + LATE,)),
        ],
        compiler_params=pltpu.CompilerParams(vmem_limit_bytes=6 << 20),
        name="release",
    )(*held)
    return following[None], volts[None], phasors.reshape(BOX, SPANS, 2, HARM)


def solution(mesh):
    return jax.shard_map(
        body,
        mesh=mesh,
        in_specs=(
            P(("region", "sub"), None, None),
            P(("region", "sub"), None, None),
            P(("region", "sub"), None),
            P(("region", "sub"), None, None, None),
            P(("region", "sub"), None, None),
            P(("region", "sub"), None, None),
            P(("region", "sub"), None),
            P(("region", "sub"), None),
            P(("region", "sub"), None, None),
        ),
        out_specs=(
            P(("region", "sub"), None, None, None),
            P(("region", "sub"), None, None),
            P(("region", "sub"), None, None, None),
        ),
        check_vma=False,
    )
```
